256 devices in a mesh: dp: 64 (over z_hi, x, y, core), fsdp: 4 (over z_lo).
Axes of the slice: x: 4, y: 4, z: 8 (z_hi: 2, z_lo: 4; z = z_hi * 4 + z_lo), core: 2. Of those that a mesh axis runs over, the one named last changes fastest.
Arguments:
- student_tiles: bfloat16 [32768, 16, 256], P(('dp', 'fsdp')), may hold values from -6 to 6
- teacher_tiles: bfloat16 [32768, 16, 512], P(('dp', 'fsdp')), may hold values from -6 to 6
- send_list: int32 [64, 4, 128], P('dp', 'fsdp'), may hold values from -1 to 127, as said below
- clip_weight: float32 [32768], P(('dp', 'fsdp')), may hold values from 0.5 to 64, as said below
- kernel_dilated: bfloat16 [1792, 256], P('fsdp'), may hold values from -0.125 to 0.125
- kernel_mix: bfloat16 [256, 256], P('fsdp'), may hold values from -0.375 to 0.375
- kernel_down: bfloat16 [4096, 512], P('fsdp'), may hold values from -0.09375 to 0.09375
- kernel_proj: bfloat16 [512, 1024], P('fsdp'), may hold values from -0.25 to 0.25
- kernel_teacher: bfloat16 [16, 512, 1024], P(None, 'fsdp'), may hold values from -0.0625 to 0.0625
- alpha_one: float32 [256], replicated, may hold values from 0.5 to 2
- alpha_two: float32 [256], replicated, may hold values from 0.5 to 2
- alpha_three: float32 [256], replicated, may hold values from 0.5 to 2
- alpha_teacher: float32 [512], replicated, may hold values from 0.5 to 2
Outputs:
- student_latent: bfloat16 [32768, 2, 1024], P(('dp', 'fsdp'))
- grad_dilated: float32 [458752], P(('dp', 'fsdp'))
- grad_mix: float32 [65536], P(('dp', 'fsdp'))
- grad_down: float32 [2097152], P(('dp', 'fsdp'))
- grad_proj: float32 [524288], P(('dp', 'fsdp'))
The draws below stay inside these ranges and needn't reach their ends.
Inputs may be any that keep to these rules, and one draw needn't show every extreme that they name: `send_list`: entries d * 2 .. d * 2 + 1 of a device's list go to dp owner d. Each device's tiles 0 .. L - 1 appear exactly once and no other tile appears, for a count L of 2 to 128 drawn per device; on every device one owner receives 2 tiles, and some device has L = 128. `clip_weight`: positive weights.
All inputs are finite; a program needn't handle non-finite values.
Results may differ from the reference program's by a relative error of at most 0.0067.
Values may be sent and summed in bfloat16 or wider, within the bound.
A program may use at most 128 MiB of HBM per device.

```python
import math
import jax
import jax.numpy as jnp
from jax import lax

CT = 512
DL = 1024
CS = 256
CSO = 512
KS = 16
STRIDE = 8
DILATED_TAPS = 7
UNIT_DILATION = 3
TILE_FRAMES = 16
TILE_DEV = 128
OUTF = 2
CAP = 2
TILES = 32768
N_DP = 64
N_FSDP = 4


def draw_send_list(key, part):
    devices_all = N_DP * N_FSDP
    key_length, key_full, key_first, key_shuffle = jax.random.split(key, 4)
    lengths = jax.random.randint(key_length, (devices_all,), CAP, TILE_DEV + 1)
    fullest = jax.random.randint(key_full, (), 0, devices_all)
    lengths = jnp.where(jnp.arange(devices_all) == fullest, TILE_DEV, lengths)
    first_owner = jax.random.randint(key_first, (devices_all,), 0, N_DP)
    shuffle = jax.vmap(lambda branch_key: jax.random.permutation(branch_key, TILE_DEV))(jax.random.split(key_shuffle, devices_all))
    position = jnp.arange(TILE_DEV)
    owner_index = position // CAP
    scores = jnp.where(owner_index[None, :] == first_owner[:, None], (position % CAP)[None, :], CAP + shuffle)
    ranking = jnp.argsort(jnp.argsort(scores, axis=1, stable=True), axis=1, stable=True)
    chosen = jnp.where(ranking < lengths[:, None], ranking, -1)
    return chosen.reshape(N_DP, N_FSDP, TILE_DEV).astype(jnp.int32)


def draw_clip_weight(key, part):
    devices_all = TILES // TILE_DEV
    base_key = jax.random.fold_in(key, 77)
    key_rank, key_rough = jax.random.split(base_key, 2)
    device_rank = jax.random.permutation(key_rank, devices_all).astype(jnp.float32)
    device_scale = 1.0 + 31.0 * jnp.power(jnp.float32(0.3), device_rank)
    rough = jnp.exp(jax.random.uniform(key_rough, (devices_all, TILE_DEV), jnp.float32, -0.693, 0.693))
    return (device_scale[:, None] * rough).reshape(-1).astype(jnp.float32)


def block_scale(stream_key, dims, cuts, low, largest):
    def one(dim, blocks):
        steps = jax.random.uniform(jax.random.fold_in(jax.random.fold_in(stream_key, 6), dim), (blocks,), jnp.float32, low / len(cuts), largest / len(cuts))
        return jnp.repeat(jnp.exp(steps), dims[dim] // blocks).reshape((-1,) + (1,) * (len(dims) - dim - 1))

    loudness = one(*cuts[0])
    for cut in cuts[1:]:
        loudness = loudness * one(*cut)
    return loudness


def centred(rng, dims, deviation, bound, cuts=(), held_as=jnp.bfloat16):
    values = jax.random.normal(rng, dims, jnp.float32) * deviation
    if len(cuts) > 0:
        values = block_scale(rng, dims, cuts, -0.22, 0.18) * values
    return jnp.clip(values, min=-bound, max=bound).astype(held_as)


def setup_inputs(seed: int = 0) -> dict:
    streams_of = jax.random.split(jax.random.key(seed), 14)
    student_tiles = centred(streams_of[0], (TILES, TILE_FRAMES, CS), 1.0, 6.0, ((0, 256),))
    teacher_tiles = centred(streams_of[1], (TILES, TILE_FRAMES, CT), 1.0, 6.0, ((0, 256),))
    send_list = draw_send_list(jax.random.fold_in(streams_of[13], 71), 0)
    clip_weight = draw_clip_weight(jax.random.fold_in(streams_of[13], 71), 0)
    kernel_dilated = centred(streams_of[4], (DILATED_TAPS * CS, CS), (DILATED_TAPS * CS) ** -0.5, 0.125, ((0, 4),))
    kernel_mix = centred(streams_of[5], (CS, CS), CS ** -0.5, 0.375, ((0, 4),))
    kernel_down = centred(streams_of[6], (KS * CS, CSO), (KS * CS) ** -0.5, 0.09375, ((0, 4),))
    kernel_proj = centred(streams_of[7], (CSO, DL), CSO ** -0.5, 0.25, ((0, 4),))
    kernel_teacher = centred(streams_of[8], (KS, CT, DL), (KS * CT) ** -0.5, 0.0625, ((1, 4),))
    alpha_one = jnp.clip(jnp.exp(jax.random.uniform(streams_of[9], (CS,), jnp.float32, math.log(0.5), math.log(2.0))), 0.5, 2.0)
    alpha_two = jnp.clip(jnp.exp(jax.random.uniform(streams_of[10], (CS,), jnp.float32, math.log(0.5), math.log(2.0))), 0.5, 2.0)
    alpha_three = jnp.clip(jnp.exp(jax.random.uniform(streams_of[11], (CS,), jnp.float32, math.log(0.5), math.log(2.0))), 0.5, 2.0)
    alpha_teacher = jnp.clip(jnp.exp(jax.random.uniform(streams_of[12], (CT,), jnp.float32, math.log(0.5), math.log(2.0))), 0.5, 2.0)
    return {"student_tiles": student_tiles, "teacher_tiles": teacher_tiles, "send_list": send_list, "clip_weight": clip_weight, "kernel_dilated": kernel_dilated, "kernel_mix": kernel_mix, "kernel_down": kernel_down, "kernel_proj": kernel_proj, "kernel_teacher": kernel_teacher, "alpha_one": alpha_one, "alpha_two": alpha_two, "alpha_three": alpha_three, "alpha_teacher": alpha_teacher}


def snake(values, alpha_vec):
    widened = values.astype(jnp.float32)
    return widened + jnp.square(jnp.sin(alpha_vec * widened)) / alpha_vec


def snake_slope(values, alpha_vec):
    return 1.0 + jnp.sin(2.0 * alpha_vec * values)


def unfold_strided(frames):
    tile_count = frames.shape[0]
    margin = (KS - STRIDE) // 2
    padded_frames = jnp.pad(frames, ((0, 0), (margin, margin), (0, 0)))
    windows = [padded_frames[:, STRIDE * offset:STRIDE * offset + KS, :].reshape(tile_count, -1) for offset in range(OUTF)]
    return jnp.stack(windows, axis=1)


def fold_strided(columns, channels):
    tile_count = columns.shape[0]
    margin = (KS - STRIDE) // 2
    padded_len = TILE_FRAMES + 2 * margin
    pieces = columns.reshape(tile_count, OUTF, KS, channels)
    folded = jnp.zeros((tile_count, padded_len, channels), jnp.float32)
    for offset in range(OUTF):
        folded = folded + jnp.pad(pieces[:, offset], ((0, 0), (STRIDE * offset, padded_len - KS - STRIDE * offset), (0, 0)))
    return folded[:, margin:margin + TILE_FRAMES, :]


def unfold_dilated(frames):
    tile_count = frames.shape[0]
    receptive_length = UNIT_DILATION * (DILATED_TAPS - 1) // 2
    padded_frames = jnp.pad(frames, ((0, 0), (receptive_length, receptive_length), (0, 0)))
    tap_offsets = [padded_frames[:, UNIT_DILATION * tap_position:UNIT_DILATION * tap_position + TILE_FRAMES, :] for tap_position in range(DILATED_TAPS)]
    return jnp.stack(tap_offsets, axis=2).reshape(tile_count * TILE_FRAMES, -1)


def teacher_forward(tiles, kernel_teacher, alpha_teacher):
    tile_count = tiles.shape[0]
    activated = snake(tiles, alpha_teacher).astype(jnp.bfloat16)
    columns = unfold_strided(activated).reshape(tile_count * OUTF, -1)
    latent = jnp.dot(columns, kernel_teacher.reshape(-1, DL), preferred_element_type=jnp.float32)
    return latent.reshape(tile_count, OUTF, DL).astype(jnp.bfloat16)


def student_step(tiles, target, weights, kernels, alphas):
    kernel_dilated, kernel_mix, kernel_down, kernel_proj = kernels
    alpha_one, alpha_two, alpha_three = alphas
    tile_count = tiles.shape[0]
    channels = tiles.shape[2]
    act_one = snake(tiles, alpha_one).astype(jnp.bfloat16)
    dilated = unfold_dilated(act_one)
    hidden = jnp.dot(dilated, kernel_dilated, preferred_element_type=jnp.float32)
    act_two = snake(hidden, alpha_two).astype(jnp.bfloat16)
    residual = tiles.reshape(tile_count * TILE_FRAMES, channels).astype(jnp.float32) + jnp.dot(act_two, kernel_mix, preferred_element_type=jnp.float32)
    act_three = snake(residual, alpha_three).astype(jnp.bfloat16).reshape(tile_count, TILE_FRAMES, channels)
    strided = unfold_strided(act_three).reshape(tile_count * OUTF, -1)
    student = jnp.dot(strided, kernel_down, preferred_element_type=jnp.float32).astype(jnp.bfloat16)
    predicted = jnp.dot(student, kernel_proj, preferred_element_type=jnp.float32)
    row_weight = jnp.repeat(weights.astype(jnp.float32), OUTF)[:, None]
    error = (row_weight * (predicted - target.reshape(tile_count * OUTF, DL).astype(jnp.float32)) / (tile_count * OUTF)).astype(jnp.bfloat16)
    grad_proj = jnp.dot(student.T, error, preferred_element_type=jnp.float32)
    back_student = jnp.dot(error, kernel_proj.T, preferred_element_type=jnp.float32).astype(jnp.bfloat16)
    grad_down = jnp.dot(strided.T, back_student, preferred_element_type=jnp.float32)
    back_columns = jnp.dot(back_student, kernel_down.T, preferred_element_type=jnp.float32).reshape(tile_count, OUTF, -1)
    back_three = fold_strided(back_columns, channels).reshape(tile_count * TILE_FRAMES, channels)
    back_residual = (back_three * snake_slope(residual, alpha_three)).astype(jnp.bfloat16)
    grad_mix = jnp.dot(act_two.T, back_residual, preferred_element_type=jnp.float32)
    back_hidden = (jnp.dot(back_residual, kernel_mix.T, preferred_element_type=jnp.float32) * snake_slope(hidden, alpha_two)).astype(jnp.bfloat16)
    grad_dilated = jnp.dot(dilated.T, back_hidden, preferred_element_type=jnp.float32)
    latent = predicted.astype(jnp.bfloat16).reshape(tile_count, OUTF, DL)
    return latent, (grad_dilated.reshape(-1), grad_mix.reshape(-1), grad_down.reshape(-1), grad_proj.reshape(-1))


def reference(student_tiles, teacher_tiles, send_list, clip_weight, kernel_dilated, kernel_mix, kernel_down, kernel_proj, kernel_teacher, alpha_one, alpha_two, alpha_three, alpha_teacher):
    devices_all = N_DP * N_FSDP
    routes = jnp.transpose(send_list.reshape(N_DP, N_FSDP, N_DP, CAP), (2, 1, 0, 3)).reshape(devices_all, TILE_DEV)
    source_dp = jnp.arange(TILE_DEV, dtype=jnp.int32) // CAP
    source_fsdp = jnp.arange(devices_all, dtype=jnp.int32) % N_FSDP
    anchor = ((source_dp[None, :] * N_FSDP + source_fsdp[:, None]) * TILE_DEV + jnp.maximum(routes, 0)).astype(jnp.int32)
    live_mask = routes >= 0
    weight_rows = clip_weight.reshape(devices_all, TILE_DEV)
    kernels = (kernel_dilated, kernel_mix, kernel_down, kernel_proj)
    alphas = (alpha_one, alpha_two, alpha_three)

    def per_device(totals, inputs):
        row_ids, used_rows, weights = inputs
        live_rows = used_rows[:, None, None]
        student_part = jnp.where(live_rows, jnp.take(student_tiles, row_ids, axis=0), jnp.zeros((), jnp.bfloat16))
        teacher_part = jnp.where(live_rows, jnp.take(teacher_tiles, row_ids, axis=0), jnp.zeros((), jnp.bfloat16))
        target = teacher_forward(teacher_part, kernel_teacher, alpha_teacher)
        latent, gradients = student_step(student_part, target, weights, kernels, alphas)
        return tuple(running + update for running, update in zip(totals, gradients)), latent

    zero_totals = tuple(jnp.zeros((kernel.size,), jnp.float32) for kernel in kernels)
    totals, latents = lax.scan(per_device, zero_totals, (anchor, live_mask, weight_rows))
    return (latents.reshape(TILES, OUTF, DL), totals[0], totals[1], totals[2], totals[3])
```

```python
import jax
import jax.numpy as jnp
import numpy as np
from jax import lax
from jax.experimental import pallas as pl
from jax.experimental.pallas import tpu as pltpu
from jax.sharding import PartitionSpec as P

BF = jnp.bfloat16
F32 = jnp.float32
MESH = pl.DeviceIdType.MESH
VMEM_LIMIT = 66_000_000


def dot(a, b):
    return jnp.dot(a, b, preferred_element_type=F32)


def dot_bt(a, b):
    return lax.dot_general(a, b, (((1,), (1,)), ((), ())), preferred_element_type=F32)


PI_PARTS = (3.125, 0.015625, 9.67502593994140625e-4, 1.509957990978376432e-7)


def fit_sin_cos():
    nodes = np.cos(np.pi * (np.arange(400) + 0.5) / 400)
    u = (nodes + 1) * 0.5 * (np.pi / 2 * 1.002) ** 2
    r = np.sqrt(u)
    sin_c = np.polynomial.polynomial.polyfit(u, np.sin(r) / r, 5)
    cos_c = np.polynomial.polynomial.polyfit(u, np.cos(r), 5)
    return [float(c) for c in sin_c], [float(c) for c in cos_c]


SIN_C, COS_C = fit_sin_cos()


def horner(u, coefs):
    acc = jnp.full_like(u, coefs[-1])
    for c in coefs[-2::-1]:
        acc = acc * u + c
    return acc


def reduce_pi(y):
    n = jnp.round(y * (1.0 / np.pi))
    r = y
    for part in PI_PARTS:
        r = r - n * part
    return r


def snake_only(v, alpha, inv):
    r = reduce_pi(alpha * v)
    s = r * horner(r * r, SIN_C)
    return v + s * s * inv


def snake_slope(v, alpha, inv):
    r = reduce_pi(alpha * v)
    u = r * r
    s = r * horner(u, SIN_C)
    c = horner(u, COS_C)
    return v + s * s * inv, 1.0 + 2.0 * s * c


def coords():
    d = lax.axis_index("dp")
    f = lax.axis_index("fsdp")
    core = d % 2
    y = (d // 2) % 4
    x = (d // 8) % 4
    zhi = d // 32
    return d, f, zhi, x, y, core


def dp_of(zhi, x, y, core):
    return ((zhi * 4 + x) * 4 + y) * 2 + core


def z_peer(zhi, f, step):
    z = (zhi * 4 + f + step + 8) % 8
    return z // 4, z % 4


class Batch:
    def __init__(self, send, recv):
        self.send, self.recv, self.next = send, recv, 0
        self.all = []

    def start(self, src, dst, device):
        copy = pltpu.make_async_remote_copy(
            src_ref=src,
            dst_ref=dst,
            send_sem=self.send.at[self.next],
            recv_sem=self.recv.at[self.next],
            device_id=device,
            device_id_type=MESH,
        )
        self.next += 1
        copy.start()
        self.all.append(copy)
        return copy

    def finish(self):
        for copy in self.all:
            copy.wait_send()


def greet(peers):
    barrier = pltpu.get_barrier_semaphore()
    for peer in peers:
        pl.semaphore_signal(barrier, inc=1, device_id=peer, device_id_type=MESH)
    pl.semaphore_wait(barrier, len(peers))


CHUNKS = 2
N_GATHER = 400


def gather_kernel(
    teach, down, proj, dil, mix, cw,
    teach_g, down_g, proj_g, dil_g, mix_g, cw_g,
    stage_t, stage_d, stage_p, stage_l, stage_m, stage_c, local_in, local_out, send, recv,
):
    d, f, zhi, x, y, core = coords()
    partner = (dp_of(zhi, x, y, 1 - core), f)
    x_peers = [(dp_of(zhi, (x + k) % 4, y, core), f) for k in (1, 2, 3)]
    y_peers = [(dp_of(zhi, x, (y + k) % 4, core), f) for k in (1, 2, 3)]
    up_h, up_f = z_peer(zhi, f, 1)
    dn_h, dn_f = z_peer(zhi, f, -1)
    far_h, far_f = z_peer(zhi, f, 2 - 4 * core)
    far2_h, far2_f = z_peer(zhi, f, 4 * core - 2)
    z_peers = [
        (dp_of(up_h, x, y, core), up_f),
        (dp_of(dn_h, x, y, core), dn_f),
        (dp_of(far_h, x, y, core), far_f),
    ]
    other = (dp_of(1 - zhi, x, y, core), f)
    remote = [(f + r) % 4 for r in (1, 2, 3)]
    own = [(teach, stage_t), (down, stage_d), (proj, stage_p), (dil, stage_l), (mix, stage_m), (cw, stage_c)]
    outs = [teach_g.at[f], down_g.at[f], proj_g.at[f], dil_g.at[f], mix_g.at[f], cw_g.at[zhi, x, y, core]]
    loads = []
    for i, (src, stage) in enumerate(own):
        loads.append(pltpu.make_async_copy(src, stage, local_in.at[i]))
        loads[-1].start()
    greet(z_peers + [(dp_of(far2_h, x, y, core), far2_f), other, partner] + x_peers + y_peers)
    b = Batch(send, recv)
    cw_z = b.start(cw, cw_g.at[zhi, x, y, core], other)

    @pl.when(core == 0)
    def _():
        pass

    chunks = [("d", None)] + [("t", c) for c in range(CHUNKS)]

    def src_piece(chunk):
        kind, c = chunk
        return down.at[x, y, core] if kind == "d" else teach.at[x, y, core, :, c]

    def piece(chunk, shard, xs, ys, cs, half):
        kind, c = chunk
        if kind == "d":
            return down_g.at[shard, xs, ys, cs, half]
        return teach_g.at[shard, xs, ys, cs, half, c]

    every = slice(None)
    z_wait = []
    for chunk in chunks:
        z_wait.append([b.start(src_piece(chunk), piece(chunk, f, x, y, core, every), peer) for peer in z_peers])
        if chunk[0] == "d":
            small = []
            for peer in z_peers:
                small.append(b.start(proj.at[core], proj_g.at[f, core], peer))
                small.append(b.start(dil.at[core], dil_g.at[f, core], peer))
                small.append(b.start(mix.at[core], mix_g.at[f, core], peer))
    to_partner = []
    cw_wait = []
    s1_wait = []
    for i, chunk in enumerate(chunks):
        for copy in z_wait[i]:
            copy.wait_recv()
        here = [[], []]
        for shard in remote:
            mine = [piece(chunk, shard, x, y, core, h) for h in (0, 1)]
            for k in range(3):
                here[0].append(b.start(mine[0], mine[0], x_peers[k]))
                here[1].append(b.start(mine[1], mine[1], y_peers[k]))
            whole = piece(chunk, shard, x, y, core, every)
            to_partner.append(b.start(whole, whole, partner))
        s1_wait.append(here)
        if i == 0:
            cw_z.wait_recv()
            line = cw_g.at[1 - zhi, x, y, core]
            cw_wait = [b.start(cw, cw_g.at[zhi, x, y, core], peer) for peer in x_peers]
            cw_wait += [b.start(line, line, peer) for peer in x_peers]
            for copy in small:
                copy.wait_recv()
            for shard in remote:
                to_partner.append(b.start(proj_g.at[shard, core], proj_g.at[shard, core], partner))
                to_partner.append(b.start(dil_g.at[shard, core], dil_g.at[shard, core], partner))
                to_partner.append(b.start(mix_g.at[shard, core], mix_g.at[shard, core], partner))
    stores = []
    for i, (src, stage) in enumerate(own):
        loads[i].wait()
        stores.append(pltpu.make_async_copy(stage, outs[i], local_out.at[i]))
        stores[-1].start()
    stores[5].wait()
    s2_wait = []
    for i, chunk in enumerate(chunks):
        here = [[], []]
        for h in (0, 1):
            for copy in s1_wait[i][h]:
                copy.wait_recv()
            for shard in remote:
                if h == 0:
                    block = piece(chunk, shard, every, y, core, 0)
                else:
                    block = piece(chunk, shard, x, every, core, 1)
                for k in range(3):
                    here[h].append(b.start(block, block, (y_peers if h == 0 else x_peers)[k]))
                for k in range(1, 4):
                    if h == 0:
                        one = piece(chunk, shard, (x + k) % 4, y, core, 0)
                    else:
                        one = piece(chunk, shard, x, (y + k) % 4, core, 1)
                    to_partner.append(b.start(one, one, partner))
        s2_wait.append(here)
        if i == 0:
            for copy in cw_wait:
                copy.wait_recv()
            block = cw_g.at[:, :, y, core]
            cw_wait = [b.start(block, block, peer) for peer in y_peers]
    for i, chunk in enumerate(chunks):
        for h in (0, 1):
            for copy in s2_wait[i][h]:
                copy.wait_recv()
            for shard in remote:
                for k in range(1, 4):
                    if h == 0:
                        one = piece(chunk, shard, every, (y + k) % 4, core, 0)
                    else:
                        one = piece(chunk, shard, (x + k) % 4, every, core, 1)
                    to_partner.append(b.start(one, one, partner))
        if i == 0:
            for copy in cw_wait:
                copy.wait_recv()
            block = cw_g.at[:, :, :, core]
            to_partner.append(b.start(block, block, partner))
    for copy in to_partner:
        copy.wait_recv()
    for copy in stores[:5]:
        copy.wait()
    b.finish()


def gather_kernels(kernel_teacher, kernel_down, kernel_proj, kernel_dilated, kernel_mix, clip_weight):
    rows = 32 // CHUNKS
    shapes = [(4, 4, 2, 2, CHUNKS, rows, 1024), (4, 4, 2, 2, 16, 512), (2, 64, 1024), (2, 224, 256), (2, 32, 256)]
    args = [
        value.reshape(shape)
        for value, shape in zip((kernel_teacher, kernel_down, kernel_proj, kernel_dilated, kernel_mix), shapes)
    ]
    cw = clip_weight.reshape(1, 128)
    outs = [jax.ShapeDtypeStruct((4,) + shape, BF) for shape in shapes]
    outs.append(jax.ShapeDtypeStruct((2, 4, 4, 2, 1, 128), F32))
    anywhere = pl.BlockSpec(memory_space=pl.ANY)
    return pl.pallas_call(
        gather_kernel,
        out_shape=outs,
        in_specs=[anywhere] * 6,
        out_specs=[anywhere] * 6,
        scratch_shapes=[pltpu.VMEM(shape, BF) for shape in shapes]
        + [
            pltpu.VMEM((1, 128), F32),
            pltpu.SemaphoreType.DMA((6,)),
            pltpu.SemaphoreType.DMA((6,)),
            pltpu.SemaphoreType.DMA((N_GATHER,)),
            pltpu.SemaphoreType.DMA((N_GATHER,)),
        ],
        compiler_params=pltpu.CompilerParams(collective_id=0, has_side_effects=True, vmem_limit_bytes=VMEM_LIMIT),
        name="gather_kernels",
    )(*args, cw)


GROUPS = ((0, 3), (3, 3), (6, 1), (7, 2), (9, 1), (10, 3), (13, 3))


def permutations():
    out = np.arange(256)
    tile = np.zeros((256, 256), np.float32)
    tile[out, (out % 16) * 16 + out // 16] = 1
    proj = np.zeros((256, 256), np.float32)
    block, m = out // 16, out % 16
    proj[out, (m % 8) * 32 + block * 2 + m // 8] = 1
    dil = np.zeros((256, 256), np.float32)
    dil[out, np.where(m < 14, (m % 2) * 112 + block * 7 + m // 2, 224 + (m - 14) * 16 + block)] = 1
    out = np.arange(512)
    lat = np.zeros((512, 512), np.float32)
    lat[out, (out % 32) * 16 + out // 32] = 1
    return [jnp.asarray(p, BF) for p in (tile, proj, dil, lat)]


def step_kernel(
    routes, weight, xs, xt, teach, down, proj, dil, mix, a1, a2, a3, at, p_tile, p_proj, p_dil, p_lat,
    lat_out, grads,
    w_t, x1s, x1t, act1, act1t, act2t, act3, act3t, act_t, hid, slope3, target, pred, error, back3, back_h, back_r,
    g_dil, stud, sems,
):
    taps = [(k if k < 16 else None) for k in (4, 5, 6, 7, 8, 9, 10, 11, 0, 12, 1, 13, 2, 14, 3, 15)]

    def tap_copy(k):
        return pltpu.make_async_copy(teach.at[:, k], w_t.at[k], sems.at[k])

    for k in taps:
        tap_copy(k).start()

    def alphas(ref):
        a = ref[...]
        return a, 1.0 / a

    @pl.loop(0, 8)
    def _(g):
        rows = pl.ds(pl.multiple_of(g * 256, 256), 256)
        cols = pl.ds(pl.multiple_of(g * 16, 16), 16)
        x1s[:, cols, :] = dot(p_tile[...], xs[rows, :]).astype(BF).reshape(16, 16, 256)
        x1t[:, cols, :] = dot(p_tile[...], xt[rows, :]).astype(BF).reshape(16, 16, 512)

    pick = jnp.where(
        routes[...] == lax.broadcasted_iota(jnp.int32, (128, 128), 1), 1.0, 0.0
    ).astype(BF)

    @pl.loop(0, 16)
    def _(j):
        value = dot(pick, x1s[j])
        x1s[j] = value.astype(BF)
        one = snake_only(value, *alphas(a1))
        act1[j] = one.astype(BF)
        act1t[j] = one.T.astype(BF)
        teacher = snake_only(dot(pick, x1t[j]), *alphas(at))
        act_t[j] = teacher.astype(BF)

    for first, count in GROUPS:
        valid = [k for k in range(7) if 0 <= first + 3 * (k - 3) <= 15]
        lhs = jnp.concatenate(
            [act1[first + 3 * (k - 3) : first + 3 * (k - 3) + count].reshape(count * 128, 256) for k in valid], axis=1
        )
        hid[first : first + count] = dot(lhs, dil[valid[0] * 256 : (valid[-1] + 1) * 256, :]).reshape(count, 128, 256)

    @pl.loop(0, 16)
    def _(j):
        act, slope = snake_slope(hid[j], *alphas(a2))
        hid[j] = slope
        act2t[j] = act.T.astype(BF)
        residual = x1s[j].astype(F32) + dot(act.astype(BF), mix[...])
        act, slope = snake_slope(residual, *alphas(a3))
        slope3[j] = slope
        act3[j] = act.astype(BF)
        act3t[j] = act.T.astype(BF)

    lhs = jnp.concatenate([jnp.concatenate([act3[k - 4], act3[k + 4]], axis=0) for k in range(4, 12)], axis=1)
    both = dot(lhs, down[1024:3072, :])
    first = dot(jnp.concatenate([act3[k] for k in range(8, 12)], axis=1), down[3072:4096, :])
    second = dot(jnp.concatenate([act3[k] for k in range(4, 8)], axis=1), down[0:1024, :])
    stud[0:128, :] = (both[0:128] + first).astype(BF)
    stud[128:256, :] = (both[128:256] + second).astype(BF)
    pred[...] = dot(stud[...], proj[...])

    target[...] = jnp.zeros_like(target)

    @pl.loop(4, 12)
    def _(k):
        tap_copy(k).wait()
        lhs = jnp.concatenate([act_t[k - 4], act_t[k + 4]], axis=0)
        target[...] += dot(lhs, w_t[k].reshape(512, 1024))

    @pl.loop(0, 4)
    def _(k):
        tap_copy(k).wait()
        target[128:256, :] += dot(act_t[k + 4], w_t[k].reshape(512, 1024))
        tap_copy(k + 12).wait()
        target[0:128, :] += dot(act_t[k + 8], w_t[k + 12].reshape(512, 1024))

    error[...] = (weight[...] * (pred[...] - target[...].astype(BF).astype(F32)) / 256.0).astype(BF)

    @pl.loop(0, 4)
    def _(g):
        parts = [
            pred[pl.ds(pl.multiple_of(o * 128 + c * 64 + g * 16, 16), 16), cb * 128 : (cb + 1) * 128].astype(BF)
            for c in range(2)
            for o in range(2)
            for cb in range(8)
        ]
        moved = dot(p_lat[...], jnp.concatenate(parts, axis=0)).astype(BF)
        lat_out[pl.ds(g * 16, 16)] = moved.reshape(16, 32, 128)

    back_s = dot_bt(error[...], proj[...]).astype(BF)

    g_proj = dot(stud[...].astype(F32).T.astype(BF), error[...])
    target[...] = g_proj[0:256]
    pred[...] = g_proj[256:512]

    @pl.loop(0, 8)
    def _(g):
        rows = pl.ds(pl.multiple_of(g * 32, 32), 32)
        for base, ref in ((0, target), (128, pred)):
            stack = jnp.concatenate([ref[rows, cb * 128 : (cb + 1) * 128].astype(BF) for cb in range(8)], axis=0)
            moved = dot(p_proj[...], stack).astype(BF).reshape(16, 16, 128)
            grads[pl.ds(base + g * 16, 16), 80:96, :] = moved

    stud[...] = back_s

    def put_down(k, value):
        for cb in range(4):
            part = value[:, cb * 128 : (cb + 1) * 128].astype(BF).reshape(16, 16, 128)
            grads[pl.ds(k * 16, 16), cb * 16 : (cb + 1) * 16, :] = part

    def tap_rows(k):
        return down[pl.ds(pl.multiple_of(k * 256, 256), 256), :]

    @pl.loop(4, 12)
    def _(k):
        put_down(k, dot(jnp.concatenate([act3t[k - 4], act3t[k + 4]], axis=1), stud[...]))
        part = dot_bt(stud[...], tap_rows(k))
        back3[k - 4] = part[0:128]
        back3[k + 4] = part[128:256]

    @pl.loop(0, 4)
    def _(k):
        put_down(k, dot(act3t[k + 4], stud[128:256, :]))
        put_down(k + 12, dot(act3t[k + 8], stud[0:128, :]))
        back3[k + 4] += dot_bt(stud[128:256, :], tap_rows(k))
        back3[k + 8] += dot_bt(stud[0:128, :], tap_rows(k + 12))

    g_dil[1792:2048, :] = jnp.zeros((256, 256), F32)

    @pl.loop(0, 16)
    def _(j):
        back = (back3[j] * slope3[j]).astype(BF)
        g_dil[1792:2048, :] += dot(act2t[j], back)
        back_h[j] = (dot_bt(back, mix[...]) * hid[j]).astype(BF)

    for k in range(7):
        shift = 3 * (k - 3)
        low, high = max(0, -shift), min(16, 16 - shift)
        lhs = jnp.concatenate([act1t[j + shift] for j in range(low, high)], axis=1)
        g_dil[k * 256 : (k + 1) * 256, :] = dot(lhs, back_h[low:high].reshape((high - low) * 128, 256))

    @pl.loop(0, 16)
    def _(g):
        rows = pl.ds(pl.multiple_of(g * 112, 16), 112)
        more = pl.ds(pl.multiple_of(1792 + g * 16, 16), 16)
        stack = jnp.concatenate(
            [g_dil[rows, 0:128], g_dil[rows, 128:256], g_dil[more, 0:128], g_dil[more, 128:256]], axis=0
        ).astype(BF)
        grads[pl.ds(g * 16, 16), 64:80, :] = dot(p_dil[...], stack).astype(BF).reshape(16, 16, 128)


def local_step(routes, weight, xs, xt, gathered, alphas):
    teach, down, proj, dil, mix = gathered
    in_vmem = pl.BlockSpec(memory_space=pltpu.VMEM)
    anywhere = pl.BlockSpec(memory_space=pl.ANY)
    frames = lambda c, t: pltpu.VMEM((16, 128, c), t)
    turned = pltpu.VMEM((16, 256, 128), BF)
    return pl.pallas_call(
        step_kernel,
        out_shape=[jax.ShapeDtypeStruct((64, 32, 128), BF), jax.ShapeDtypeStruct((256, 96, 128), BF)],
        in_specs=[in_vmem] * 4 + [anywhere] + [in_vmem] * 12,
        out_specs=[in_vmem] * 2,
        scratch_shapes=[
            pltpu.VMEM((16, 4, 128, 1024), BF),
            frames(256, BF), frames(512, BF), frames(256, BF), turned, turned, frames(256, BF), turned,
            frames(512, BF), frames(256, F32), frames(256, F32),
            pltpu.VMEM((256, 1024), F32), pltpu.VMEM((256, 1024), F32), pltpu.VMEM((256, 1024), BF),
            frames(256, F32), frames(256, BF), pltpu.VMEM((8, 128), BF),
            pltpu.VMEM((2048, 256), F32), pltpu.VMEM((256, 512), BF), pltpu.SemaphoreType.DMA((16,)),
        ],
        compiler_params=pltpu.CompilerParams(vmem_limit_bytes=VMEM_LIMIT),
        name="local_step",
    )(routes, weight, xs, xt, teach, down, proj, dil, mix, *alphas, *permutations())


def exchange_kernel(
    lat, grads, lat_g, total,
    r0, s1, r1, s2, r2, s3, r3, lat_sem, own_sem, send, recv,
):
    d, f, zhi, x, y, core = coords()
    partner = (dp_of(zhi, x, y, 1 - core), f)
    x_peers = [(dp_of(zhi, (x + k) % 4, y, core), f) for k in (1, 2, 3)]
    y_peers = [(dp_of(zhi, x, (y + k) % 4, core), f) for k in (1, 2, 3)]
    z_ids = [z_peer(zhi, f, k) for k in range(1, 8)]
    z_peers = [(dp_of(h, x, y, core), g) for h, g in z_ids]
    barrier = pltpu.get_barrier_semaphore()

    def hello(k, carry):
        pl.semaphore_signal(barrier, inc=1, device_id=((d + k) % 64, f), device_id_type=MESH)
        return carry

    lax.fori_loop(1, 64, hello, 0)
    for k, peer in enumerate(z_peers):
        if k != 3:
            pl.semaphore_signal(barrier, inc=1, device_id=peer, device_id_type=MESH)
    pl.semaphore_wait(barrier, 63 + 6)

    own = pltpu.make_async_copy(lat.at[d], lat_g.at[d], own_sem)
    own.start()
    b = Batch(send, recv)
    pieces = [[], []]
    order = (1, 2, 3, 0)
    for k in order:
        for h in (0, 1):
            if h == 0:
                src = grads.at[:, (x + k) % 4, :, 1 - core, :, 0]
            else:
                src = grads.at[:, :, (y + k) % 4, 1 - core, :, 1]
            pieces[h].append(b.start(src, r0.at[h, k], partner))

    def lat_copy(k):
        to = (d + k) % 64
        return pltpu.make_async_remote_copy(
            src_ref=lat.at[to], dst_ref=lat_g.at[d], send_sem=lat_sem.at[0, k - 1], recv_sem=lat_sem.at[1, k - 1],
            device_id=(to, f), device_id_type=MESH,
        )

    first = [[], []]
    for i, k in enumerate(order):
        for h in (0, 1):
            pieces[h][i].wait_recv()

            @pl.loop(0, 8)
            def _(n):
                if h == 0:
                    mine = grads[n // 4, (x + k) % 4, n % 4, core, :, 0]
                else:
                    mine = grads[n // 4, n % 4, (y + k) % 4, core, :, 1]
                s1[h, k, n // 4, n % 4] = (mine.astype(F32) + r0[h, k, n // 4, n % 4].astype(F32)).astype(BF)

            if k > 0:
                first[h].append(b.start(s1.at[h, k], r1.at[h, k - 1], (x_peers, y_peers)[h][k - 1]))

    def send_lat(k, carry):
        lat_copy(k).start()
        return carry

    lax.fori_loop(1, 64, send_lat, 0)

    second = [[], []]
    for h in (0, 1):
        for copy in first[h]:
            copy.wait_recv()

        @pl.loop(0, 8)
        def _(n):
            a, e = n // 4, n % 4
            acc = s1[h, 0, a, e].astype(F32)
            for k in range(3):
                acc = acc + r1[h, k, a, e].astype(F32)
            s2[h, e, a] = acc.astype(BF)

        mine = (y, x)[h]
        for k in (1, 2, 3):
            second[h].append(b.start(s2.at[h, (mine + k) % 4], r2.at[h, k - 1], (y_peers, x_peers)[h][k - 1]))
    third = [[], []]
    for h in (0, 1):
        for copy in second[h]:
            copy.wait_recv()
        mine = (y, x)[h]

        @pl.loop(0, 2)
        def _(a):
            acc = s2[h, mine, a].astype(F32)
            for k in range(3):
                acc = acc + r2[h, k, a].astype(F32)
            s3[h, a] = acc.astype(BF)

        for k in range(7):
            zh, zf = z_ids[k]
            third[h].append(b.start(s3.at[h, zh, zf], r3.at[h, k], z_peers[k]))
    for h in (0, 1):
        for copy in third[h]:
            copy.wait_recv()
        acc = s3[h, zhi, f].astype(F32)
        for k in range(7):
            acc = acc + r3[h, k].astype(F32)
        total[h] = acc
    own.wait()

    def wait_lat(k, carry):
        copy = lat_copy(k)
        copy.wait_recv()
        copy.wait_send()
        return carry

    lax.fori_loop(1, 64, wait_lat, 0)
    b.finish()


def exchange(lat, grads):
    in_vmem = pl.BlockSpec(memory_space=pltpu.VMEM)
    block = (48, 128)
    copies = 8 + 6 + 6 + 14
    return pl.pallas_call(
        exchange_kernel,
        out_shape=[jax.ShapeDtypeStruct((64, 32, 128), BF), jax.ShapeDtypeStruct((2, 48, 128), F32)],
        in_specs=[in_vmem] * 2,
        out_specs=[in_vmem] * 2,
        scratch_shapes=[
            pltpu.VMEM((2, 4, 2, 4, 4) + block, BF),
            pltpu.VMEM((2, 4, 2, 4, 4) + block, BF),
            pltpu.VMEM((2, 3, 2, 4, 4) + block, BF),
            pltpu.VMEM((2, 4, 2, 4) + block, BF),
            pltpu.VMEM((2, 3, 2, 4) + block, BF),
            pltpu.VMEM((2, 2, 4) + block, BF),
            pltpu.VMEM((2, 7) + block, BF),
            pltpu.SemaphoreType.DMA((2, 63)),
            pltpu.SemaphoreType.DMA,
            pltpu.SemaphoreType.DMA((copies,)),
            pltpu.SemaphoreType.DMA((copies,)),
        ],
        compiler_params=pltpu.CompilerParams(collective_id=1, has_side_effects=True, vmem_limit_bytes=VMEM_LIMIT),
        name="exchange",
    )(lat, grads.reshape((2, 4, 4, 2, 4, 2) + block))


def on_device(
    student_tiles, teacher_tiles, send_list, clip_weight, kernel_dilated, kernel_mix, kernel_down, kernel_proj,
    kernel_teacher, alpha_one, alpha_two, alpha_three, alpha_teacher,
):
    teach, down, proj, dil, mix, cw = gather_kernels(
        kernel_teacher, kernel_down, kernel_proj, kernel_dilated, kernel_mix, clip_weight
    )
    gathered = (
        teach.reshape(4, 16, 128, 1024), down.reshape(4096, 512), proj.reshape(512, 1024),
        dil.reshape(1792, 256), mix.reshape(256, 256),
    )
    d = lax.axis_index("dp")
    routes = send_list.reshape(64, 2).T.reshape(128, 1)
    weight = lax.dynamic_slice(cw.reshape(64, 128), (0, 2 * d), (64, 2)).T.reshape(128, 1)
    lat, grads = local_step(
        routes,
        jnp.concatenate([weight, weight], axis=0),
        student_tiles.reshape(2048, 256),
        teacher_tiles.reshape(2048, 512),
        gathered,
        [a.reshape(1, -1) for a in (alpha_one, alpha_two, alpha_three, alpha_teacher)],
    )
    lat, total = exchange(lat, grads)
    total = total.reshape(96, 128)
    g_down = total[0:64].reshape(4, 16, 128).transpose(1, 0, 2).reshape(-1)
    return (
        lat.reshape(128, 2, 1024),
        total[64:80][0:14].reshape(-1),
        total[78:80].reshape(-1),
        g_down,
        total[80:96].reshape(-1),
    )


def solution(mesh):
    both = P(("dp", "fsdp"))
    return jax.shard_map(
        on_device,
        mesh=mesh,
        in_specs=(
            P(("dp", "fsdp"), None, None),
            P(("dp", "fsdp"), None, None),
            P("dp", "fsdp", None),
            both,
            P("fsdp", None),
            P("fsdp", None),
            P("fsdp", None),
            P("fsdp", None),
            P(None, "fsdp", None),
            P(),
            P(),
            P(),
            P(),
        ),
        out_specs=(P(("dp", "fsdp"), None, None), both, both, both, both),
        check_vma=False,
    )
```

```python
import jax
import jax.numpy as jnp
import numpy as np
from jax import lax
from jax.experimental import pallas as pl
from jax.experimental.pallas import tpu as pltpu
from jax.sharding import PartitionSpec as P

BF = jnp.bfloat16
F32 = jnp.float32
MESH = pl.DeviceIdType.MESH
VMEM_LIMIT = 66_000_000


def dot(a, b):
    return jnp.dot(a, b, preferred_element_type=F32)


def dot_bt(a, b):
    return lax.dot_general(a, b, (((1,), (1,)), ((), ())), preferred_element_type=F32)


PI_PARTS = (3.125, 0.015625, 9.67502593994140625e-4, 1.509957990978376432e-7)


def fit_sin_cos():
    nodes = np.cos(np.pi * (np.arange(400) + 0.5) / 400)
    u = (nodes + 1) * 0.5 * (np.pi / 2 * 1.002) ** 2
    r = np.sqrt(u)
    sin_c = np.polynomial.polynomial.polyfit(u, np.sin(r) / r, 5)
    cos_c = np.polynomial.polynomial.polyfit(u, np.cos(r), 5)
    return [float(c) for c in sin_c], [float(c) for c in cos_c]


SIN_C, COS_C = fit_sin_cos()


def horner(u, coefs):
    acc = jnp.full_like(u, coefs[-1])
    for c in coefs[-2::-1]:
        acc = acc * u + c
    return acc


def reduce_pi(y):
    n = jnp.round(y * (1.0 / np.pi))
    r = y
    for part in PI_PARTS:
        r = r - n * part
    return r


def snake_only(v, alpha, inv):
    r = reduce_pi(alpha * v)
    s = r * horner(r * r, SIN_C)
    return v + s * s * inv


def snake_slope(v, alpha, inv):
    r = reduce_pi(alpha * v)
    u = r * r
    s = r * horner(u, SIN_C)
    c = horner(u, COS_C)
    return v + s * s * inv, 1.0 + 2.0 * s * c


def coords():
    d = lax.axis_index("dp")
    f = lax.axis_index("fsdp")
    core = d % 2
    y = (d // 2) % 4
    x = (d // 8) % 4
    zhi = d // 32
    return d, f, zhi, x, y, core


def dp_of(zhi, x, y, core):
    return ((zhi * 4 + x) * 4 + y) * 2 + core


def z_peer(zhi, f, step):
    z = (zhi * 4 + f + step + 8) % 8
    return z // 4, z % 4


class Batch:
    def __init__(self, send, recv):
        self.send, self.recv, self.next = send, recv, 0
        self.all = []

    def start(self, src, dst, device):
        copy = pltpu.make_async_remote_copy(
            src_ref=src,
            dst_ref=dst,
            send_sem=self.send.at[self.next],
            recv_sem=self.recv.at[self.next],
            device_id=device,
            device_id_type=MESH,
        )
        self.next += 1
        copy.start()
        self.all.append(copy)
        return copy

    def finish(self):
        for copy in self.all:
            copy.wait_send()


GROUPS = ((0, 3), (3, 3), (6, 1), (7, 2), (9, 1), (10, 3), (13, 3))


def permutations():
    out = np.arange(256)
    tile = np.zeros((256, 256), np.float32)
    tile[out, (out % 16) * 16 + out // 16] = 1
    proj = np.zeros((256, 256), np.float32)
    block, m = out // 16, out % 16
    proj[out, (m % 8) * 32 + block * 2 + m // 8] = 1
    dil = np.zeros((256, 256), np.float32)
    dil[out, np.where(m < 14, (m % 2) * 112 + block * 7 + m // 2, 224 + (m - 14) * 16 + block)] = 1
    out = np.arange(512)
    lat = np.zeros((512, 512), np.float32)
    lat[out, (out % 32) * 16 + out // 32] = 1
    return [jnp.asarray(p, BF) for p in (tile, proj, dil, lat)]


EVERY = slice(None)
N_COPIES = 260


class Chunk:
    def __init__(self, batch, place, remote, peers, number, source, view):
        self.b, self.place, self.remote, self.number = batch, place, remote, number
        self.source, self.view = source, view
        self.peers = peers

    def start(self, own, z_peers):
        x, y = self.place
        self.z = [self.b.start(self.source, self.view(own, x, y, EVERY), peer) for peer in z_peers]

    def line(self, shard, along, step, wide, cut=EVERY):
        x, y = self.place
        half = along if not wide else 1 - along
        if along == 0:
            return self.view(shard, (x + step) % 4, cut if wide else y, half)
        return self.view(shard, cut if wide else x, (y + step) % 4, half)

    def z_done(self):
        for copy in self.z:
            copy.wait_recv()
        self.direct = []
        for along in (0, 1):
            for shard in self.remote:
                ref = self.line(shard, along, 0, False)
                for step in (1, -1):
                    self.direct.append(self.b.start(ref, ref, self.peers[along][step]))

    def first_relay(self):
        for copy in self.direct:
            copy.wait_recv()
        self.relay = []
        for along in (0, 1):
            for i, shard in enumerate(self.remote):
                step = 1 if (self.number + i + along) % 2 == 0 else -1
                ref = self.line(shard, along, -step, False)
                self.relay.append(self.b.start(ref, ref, self.peers[along][step]))

    def first_done(self):
        for copy in self.relay:
            copy.wait_recv()
        self.direct = []
        for along in (0, 1):
            for shard in self.remote:
                ref = self.line(shard, along, 0, True)
                for step in (1, -1):
                    self.direct.append(self.b.start(ref, ref, self.peers[along][step]))

    def second_relay(self):
        for copy in self.direct:
            copy.wait_recv()
        self.relay = []
        for along in (0, 1):
            for shard in self.remote:
                for step, cut in ((1, slice(0, 2)), (-1, slice(2, 4))):
                    ref = self.line(shard, along, -step, True, cut)
                    self.relay.append(self.b.start(ref, ref, self.peers[along][step]))

    def second_done(self):
        for copy in self.relay:
            copy.wait_recv()


def whole_kernel(
    teach_in, down_in, proj_in, dil_in, mix_in, cw_in, routes, xs, xt, a1, a2, a3, at, p_tile, p_proj, p_dil, p_lat,
    lat_g, total,
    w_t, w_d, w_p, w_l, w_m, cw, x1s, x1t, act1, act1t, act2t, act3, act3t, act_t, act_p, hid, slope3,
    tacc, tsend, targ, pred, error, back3, back_h, g_dil, stud, lat, grads, r0, s1, r1, s2, r2, s3, r3,
    local_sem, lat_sem, own_sem, send, recv,
):
    d, f, zhi, x, y, core = coords()
    partner = (dp_of(zhi, x, y, 1 - core), f)
    x_peers = [(dp_of(zhi, (x + k) % 4, y, core), f) for k in (1, 2, 3)]
    y_peers = [(dp_of(zhi, x, (y + k) % 4, core), f) for k in (1, 2, 3)]
    z_ids = [z_peer(zhi, f, k) for k in range(1, 8)]
    z_all = [(dp_of(h, x, y, core), g) for h, g in z_ids]
    far_h, far_f = z_peer(zhi, f, 2 - 4 * core)
    z_near = [z_all[0], z_all[6], (dp_of(far_h, x, y, core), far_f)]
    other = z_all[3]
    remote = [(f + r) % 4 for r in (1, 2, 3)]

    def columns(c):
        return pl.ds(pl.multiple_of(core * 512 + c * 256, 256), 256)

    loads = [
        (dil_in, w_l.at[f]), (mix_in, w_m.at[f]), (down_in, w_d.at[f]), (proj_in, w_p.at[f]),
        (cw_in, cw.at[zhi, x, y, core]),
    ]
    loads += [(teach_in.at[:, :, :, :, columns(c)], w_t.at[c, f]) for c in (0, 1)]
    loads = [pltpu.make_async_copy(src, dst, local_sem.at[i]) for i, (src, dst) in enumerate(loads)]
    for copy in loads:
        copy.start()

    barrier = pltpu.get_barrier_semaphore()
    for k, peer in enumerate(z_all):
        if k != 3:
            pl.semaphore_signal(barrier, inc=1, device_id=peer, device_id_type=MESH)

    def hello(k, carry):
        pl.semaphore_signal(barrier, inc=1, device_id=((d + k) % 64, f), device_id_type=MESH)
        return carry

    lax.fori_loop(1, 64, hello, 0)
    pl.semaphore_wait(barrier, 63 + 6)

    b = Batch(send, recv)
    peers = ({1: x_peers[0], -1: x_peers[2]}, {1: y_peers[0], -1: y_peers[2]})
    small = []
    for peer in z_near:
        small.append(b.start(dil_in.at[core], w_l.at[f, core], peer))
        small.append(b.start(mix_in.at[core], w_m.at[f, core], peer))
    cw_wait = [b.start(cw_in, cw.at[zhi, x, y, core], other)]
    cd = Chunk(b, (x, y), remote, peers, 0, down_in.at[x, y, core], lambda s, i, j, h: w_d.at[s, i, j, core, h])
    c0 = Chunk(
        b, (x, y), remote, peers, 1, teach_in.at[x, y, :, :, columns(0)], lambda s, i, j, h: w_t.at[0, s, i, j, h]
    )
    c1 = Chunk(
        b, (x, y), remote, peers, 0, teach_in.at[x, y, :, :, columns(1)], lambda s, i, j, h: w_t.at[1, s, i, j, h]
    )
    for chunk in (cd, c0, c1):
        chunk.start(f, z_near)
    small_p = [b.start(proj_in.at[core], w_p.at[f, core], peer) for peer in z_near]

    def alphas(ref):
        a = ref[...]
        return a, 1.0 / a

    @pl.loop(0, 8)
    def _(g):
        rows = pl.ds(pl.multiple_of(g * 256, 256), 256)
        cols = pl.ds(pl.multiple_of(g * 16, 16), 16)
        x1s[:, cols, :] = dot(p_tile[...], xs[rows, :]).astype(BF).reshape(16, 16, 256)
        x1t[:, cols, :] = dot(p_tile[...], xt[rows, :]).astype(BF).reshape(16, 16, 512)

    pick = jnp.where(
        routes[...] == lax.broadcasted_iota(jnp.int32, (128, 128), 1), 1.0, 0.0
    ).astype(BF)

    def teacher_act(low, high):
        @pl.loop(low, high)
        def _(j):
            act_t[j] = snake_only(dot(pick, x1t[j]), *alphas(at)).astype(BF)

    for chunk in (cd, c0, c1):
        chunk.z_done()
    for copy in small:
        copy.wait_recv()
    to_partner = []
    for shard in remote:
        to_partner.append(b.start(w_l.at[shard, core], w_l.at[shard, core], partner))
        to_partner.append(b.start(w_m.at[shard, core], w_m.at[shard, core], partner))
    loads[4].wait()
    for copy in cw_wait:
        copy.wait_recv()
    block = cw.at[:, x, y, core]
    cw_wait = [b.start(block, block, peer) for peer in x_peers]
    teacher_act(0, 8)
    for chunk in (cd, c0, c1):
        chunk.first_relay()
    teacher_act(8, 16)
    act_copy = b.start(act_t, act_p, partner)
    cd.first_done()
    c0.first_done()
    for copy in cw_wait:
        copy.wait_recv()
    block = cw.at[:, :, y, core]
    cw_wait = [b.start(block, block, peer) for peer in y_peers]
    for copy in small_p:
        copy.wait_recv()
    proj_copies = [b.start(w_p.at[shard, core], w_p.at[shard, core], partner) for shard in remote]
    c1.first_done()

    @pl.loop(0, 16)
    def _(j):
        value = dot(pick, x1s[j])
        x1s[j] = value.astype(BF)
        one = snake_only(value, *alphas(a1))
        act1[j] = one.astype(BF)
        act1t[j] = one.T.astype(BF)

    cd.second_relay()
    for copy in loads[0:2] :
        copy.wait()
    for copy in to_partner:
        copy.wait_recv()
    c0.second_relay()

    w_dil = w_l[...].reshape(1792, 256)
    for first, count in GROUPS:
        valid = [k for k in range(7) if 0 <= first + 3 * (k - 3) <= 15]
        lhs = jnp.concatenate(
            [act1[first + 3 * (k - 3) : first + 3 * (k - 3) + count].reshape(count * 128, 256) for k in valid], axis=1
        )
        hid[first : first + count] = dot(lhs, w_dil[valid[0] * 256 : (valid[-1] + 1) * 256, :]).reshape(count, 128, 256)
    cd.second_done()
    down_copies = [b.start(w_d.at[shard, :, :, core], w_d.at[shard, :, :, core], partner) for shard in remote]
    for copy in cw_wait:
        copy.wait_recv()
    block = cw.at[:, :, :, core]
    cw_wait = [b.start(block, block, partner)]

    @pl.loop(0, 16)
    def _(j):
        act, slope = snake_slope(hid[j], *alphas(a2))
        hid[j] = slope
        act2t[j] = act.T.astype(BF)
        residual = x1s[j].astype(F32) + dot(act.astype(BF), w_m[...].reshape(256, 256))
        act, slope = snake_slope(residual, *alphas(a3))
        slope3[j] = slope
        act3[j] = act.astype(BF)
        act3t[j] = act.T.astype(BF)

    c1.second_relay()

    for copy in down_copies + proj_copies:
        copy.wait_recv()
    for copy in loads[2:4]:
        copy.wait()

    def tap_rows(k):
        return w_d[k // 4, k % 4].reshape(256, 512)

    def shard_rows(s):
        return w_d[s].reshape(1024, 512)

    lhs = jnp.concatenate([jnp.concatenate([act3[k - 4], act3[k + 4]], axis=0) for k in range(4, 12)], axis=1)
    both = dot(lhs, w_d[1:3].reshape(2048, 512))
    first = dot(jnp.concatenate([act3[k] for k in range(8, 12)], axis=1), shard_rows(3))
    second = dot(jnp.concatenate([act3[k] for k in range(4, 8)], axis=1), shard_rows(0))
    stud[0:128, :] = (both[0:128] + first).astype(BF)
    stud[128:256, :] = (both[128:256] + second).astype(BF)
    w_proj = w_p[...].reshape(512, 1024)
    pred[...] = dot(stud[...], w_proj)

    @pl.loop(0, 4)
    def _(g):
        parts = [
            pred[pl.ds(pl.multiple_of(o * 128 + c * 64 + g * 16, 16), 16), cb * 128 : (cb + 1) * 128].astype(BF)
            for c in range(2)
            for o in range(2)
            for cb in range(8)
        ]
        moved = dot(p_lat[...], jnp.concatenate(parts, axis=0)).astype(BF)
        lat[pl.ds(g * 16, 16)] = moved.reshape(16, 32, 128)

    act_copy.wait_recv()
    target_copies = []
    for c, chunk in ((0, c0), (1, c1)):
        chunk.second_done()
        loads[5 + c].wait()
        tacc[...] = jnp.zeros_like(tacc)

        @pl.loop(4, 12)
        def _(k):
            lhs = jnp.concatenate([act_t[k - 4], act_p[k - 4], act_t[k + 4], act_p[k + 4]], axis=0)
            tacc[...] += dot(lhs, w_t[c, :, k // 4, k % 4].reshape(512, 256))

        @pl.loop(0, 4)
        def _(k):
            lhs = jnp.concatenate([act_t[k + 4], act_p[k + 4]], axis=0)
            tacc[256:512, :] += dot(lhs, w_t[c, :, 0, k].reshape(512, 256))
            lhs = jnp.concatenate([act_t[k + 8], act_p[k + 8]], axis=0)
            tacc[0:256, :] += dot(lhs, w_t[c, :, 3, k].reshape(512, 256))

        tsend[c, 0:128] = tacc[128:256, :].astype(BF)
        tsend[c, 128:256] = tacc[384:512, :].astype(BF)
        targ[core, c, 0:128] = tacc[0:128, :].astype(BF)
        targ[core, c, 128:256] = tacc[256:384, :].astype(BF)
        target_copies.append(b.start(tsend.at[c], targ.at[core, c], partner))

    own = pltpu.make_async_copy(lat.at[d], lat_g.at[d], own_sem)
    own.start()

    def lat_copy(k):
        to = (d + k) % 64
        return pltpu.make_async_remote_copy(
            src_ref=lat.at[to], dst_ref=lat_g.at[d], send_sem=lat_sem.at[0, k - 1], recv_sem=lat_sem.at[1, k - 1],
            device_id=(to, f), device_id_type=MESH,
        )

    def send_lat(k, carry):
        lat_copy(k).start()
        return carry

    lax.fori_loop(1, 64, send_lat, 0)

    for copy in cw_wait + target_copies:
        copy.wait_recv()
    lines = cw[...].reshape(64, 128)
    lane = lax.broadcasted_iota(jnp.int32, (64, 128), 1)
    pair = [jnp.sum(jnp.where(lane == 2 * d + c, lines, 0.0), axis=1, keepdims=True) for c in (0, 1)]
    weight = jnp.concatenate(pair + pair, axis=0)
    for cc in (0, 1):
        for c in (0, 1):
            cols = slice((cc * 2 + c) * 256, (cc * 2 + c + 1) * 256)
            error[:, cols] = (weight * (pred[:, cols] - targ[cc, c].astype(F32)) / 256.0).astype(BF)

    back_s = dot_bt(error[...], w_proj).astype(BF)

    def put(k, half, row, value):
        grads[k // 8, (k // 2) % 4, pl.ds((k % 2) * 2, 2), :, :, half, row : row + 16, :] = value.astype(BF).reshape(
            2, 2, 4, 16, 128
        )

    g_proj = dot(stud[...].astype(F32).T.astype(BF), error[...])
    pred[...] = g_proj[0:256]
    g_dil[0:1024, :] = jnp.concatenate([g_proj[256:512, i * 256 : (i + 1) * 256] for i in range(4)], axis=0)

    @pl.loop(0, 8)
    def _(g):
        low = [pred[pl.ds(pl.multiple_of(g * 32, 32), 32), i * 128 : (i + 1) * 128] for i in range(8)]
        high = [
            g_dil[pl.ds(pl.multiple_of((i // 2) * 256 + g * 32, 32), 32), (i % 2) * 128 : (i % 2 + 1) * 128]
            for i in range(8)
        ]
        for base, parts in ((0, low), (8, high)):
            put(base + g, 1, 32, dot(p_proj[...], jnp.concatenate(parts, axis=0).astype(BF)))

    stud[...] = back_s

    def put_down(k, value):
        for cb in range(4):
            put(k, cb // 3, (cb % 3) * 16, value[:, cb * 128 : (cb + 1) * 128])

    @pl.loop(4, 12)
    def _(k):
        put_down(k, dot(jnp.concatenate([act3t[k - 4], act3t[k + 4]], axis=1), stud[...]))
        part = dot_bt(stud[...], tap_rows(k))
        back3[k - 4] = part[0:128]
        back3[k + 4] = part[128:256]

    @pl.loop(0, 4)
    def _(k):
        put_down(k, dot(act3t[k + 4], stud[128:256, :]))
        put_down(k + 12, dot(act3t[k + 8], stud[0:128, :]))
        back3[k + 4] += dot_bt(stud[128:256, :], tap_rows(k))
        back3[k + 8] += dot_bt(stud[0:128, :], tap_rows(k + 12))

    order = (1, 2, 3, 0)
    pieces = [[], []]

    def to_core(h):
        for k in order:
            if h == 0:
                src = grads.at[:, (x + k) % 4, :, 1 - core, :, 0]
            else:
                src = grads.at[:, :, (y + k) % 4, 1 - core, :, 1]
            pieces[h].append(b.start(src, r0.at[h, k], partner))

    to_core(0)
    g_dil[1792:2048, :] = jnp.zeros((256, 256), F32)

    @pl.loop(0, 16)
    def _(j):
        back = (back3[j] * slope3[j]).astype(BF)
        g_dil[1792:2048, :] += dot(act2t[j], back)
        back_h[j] = (dot_bt(back, w_m[...].reshape(256, 256)) * hid[j]).astype(BF)

    first = [[], []]

    def sum_cores(h):
        for i, k in enumerate(order):
            pieces[h][i].wait_recv()

            @pl.loop(0, 8)
            def _(n):
                if h == 0:
                    mine = grads[n // 4, (x + k) % 4, n % 4, core, :, 0]
                else:
                    mine = grads[n // 4, n % 4, (y + k) % 4, core, :, 1]
                s1[h, k, n // 4, n % 4] = (mine.astype(F32) + r0[h, k, n // 4, n % 4].astype(F32)).astype(BF)

            if k > 0:
                first[h].append(b.start(s1.at[h, k], r1.at[h, k - 1], (x_peers, y_peers)[h][k - 1]))

    sum_cores(0)
    for k in range(7):
        shift = 3 * (k - 3)
        low, high = max(0, -shift), min(16, 16 - shift)
        lhs = jnp.concatenate([act1t[j + shift] for j in range(low, high)], axis=1)
        g_dil[k * 256 : (k + 1) * 256, :] = dot(lhs, back_h[low:high].reshape((high - low) * 128, 256))

    @pl.loop(0, 16)
    def _(g):
        rows = pl.ds(pl.multiple_of(g * 112, 16), 112)
        more = pl.ds(pl.multiple_of(1792 + g * 16, 16), 16)
        stack = jnp.concatenate(
            [g_dil[rows, 0:128], g_dil[rows, 128:256], g_dil[more, 0:128], g_dil[more, 128:256]], axis=0
        ).astype(BF)
        put(g, 1, 16, dot(p_dil[...], stack))

    to_core(1)
    sum_cores(1)

    second = [[], []]
    for h in (0, 1):
        for copy in first[h]:
            copy.wait_recv()

        @pl.loop(0, 8)
        def _(n):
            a, e = n // 4, n % 4
            acc = s1[h, 0, a, e].astype(F32)
            for k in range(3):
                acc = acc + r1[h, k, a, e].astype(F32)
            s2[h, e, a] = acc.astype(BF)

        mine = (y, x)[h]
        for k in (1, 2, 3):
            second[h].append(b.start(s2.at[h, (mine + k) % 4], r2.at[h, k - 1], (y_peers, x_peers)[h][k - 1]))
    third = [[], []]
    for h in (0, 1):
        for copy in second[h]:
            copy.wait_recv()
        mine = (y, x)[h]

        @pl.loop(0, 2)
        def _(a):
            acc = s2[h, mine, a].astype(F32)
            for k in range(3):
                acc = acc + r2[h, k, a].astype(F32)
            s3[h, a] = acc.astype(BF)

        for k in range(7):
            zh, zf = z_ids[k]
            third[h].append(b.start(s3.at[h, zh, zf], r3.at[h, k], z_all[k]))
    for h in (0, 1):
        for copy in third[h]:
            copy.wait_recv()
        acc = s3[h, zhi, f].astype(F32)
        for k in range(7):
            acc = acc + r3[h, k].astype(F32)
        total[h] = acc
    own.wait()

    def wait_lat(k, carry):
        copy = lat_copy(k)
        copy.wait_recv()
        copy.wait_send()
        return carry

    lax.fori_loop(1, 64, wait_lat, 0)
    b.finish()


def whole(teach, down, proj, dil, mix, clip_weight, routes, xs, xt, alphas):
    in_vmem = pl.BlockSpec(memory_space=pltpu.VMEM)
    anywhere = pl.BlockSpec(memory_space=pl.ANY)
    frames = lambda c, t: pltpu.VMEM((16, 128, c), t)
    turned = pltpu.VMEM((16, 256, 128), BF)
    block = (48, 128)
    args = [
        teach.reshape(4, 4, 2, 64, 1024),
        down.reshape(4, 4, 2, 2, 16, 512),
        proj.reshape(2, 64, 1024),
        dil.reshape(2, 224, 256),
        mix.reshape(2, 32, 256),
        clip_weight.reshape(1, 128),
    ]
    return pl.pallas_call(
        whole_kernel,
        out_shape=[jax.ShapeDtypeStruct((64, 32, 128), BF), jax.ShapeDtypeStruct((2,) + block, F32)],
        in_specs=[anywhere] * 6 + [in_vmem] * 11,
        out_specs=[in_vmem] * 2,
        scratch_shapes=[
            pltpu.VMEM((2, 4, 4, 4, 2, 64, 256), BF),
            pltpu.VMEM((4, 4, 4, 2, 2, 16, 512), BF),
            pltpu.VMEM((4, 2, 64, 1024), BF),
            pltpu.VMEM((4, 2, 224, 256), BF),
            pltpu.VMEM((4, 2, 32, 256), BF),
            pltpu.VMEM((2, 4, 4, 2, 1, 128), F32),
            frames(256, BF), frames(512, BF), frames(256, BF), turned, turned, frames(256, BF), turned,
            frames(512, BF), frames(512, BF), frames(256, F32), frames(256, F32),
            pltpu.VMEM((512, 256), F32), pltpu.VMEM((2, 256, 256), BF), pltpu.VMEM((2, 2, 256, 256), BF),
            pltpu.VMEM((256, 1024), F32), pltpu.VMEM((256, 1024), BF),
            frames(256, F32), frames(256, BF),
            pltpu.VMEM((2048, 256), F32), pltpu.VMEM((256, 512), BF),
            pltpu.VMEM((64, 32, 128), BF), pltpu.VMEM((2, 4, 4, 2, 4, 2) + block, BF),
            pltpu.VMEM((2, 4, 2, 4, 4) + block, BF),
            pltpu.VMEM((2, 4, 2, 4, 4) + block, BF),
            pltpu.VMEM((2, 3, 2, 4, 4) + block, BF),
            pltpu.VMEM((2, 4, 2, 4) + block, BF),
            pltpu.VMEM((2, 3, 2, 4) + block, BF),
            pltpu.VMEM((2, 2, 4) + block, BF),
            pltpu.VMEM((2, 7) + block, BF),
            pltpu.SemaphoreType.DMA((7,)),
            pltpu.SemaphoreType.DMA((2, 63)),
            pltpu.SemaphoreType.DMA,
            pltpu.SemaphoreType.DMA((N_COPIES,)),
            pltpu.SemaphoreType.DMA((N_COPIES,)),
        ],
        compiler_params=pltpu.CompilerParams(collective_id=0, has_side_effects=True, vmem_limit_bytes=VMEM_LIMIT),
        name="whole_step",
    )(*args, routes, xs, xt, *alphas, *permutations())


def on_device(
    student_tiles, teacher_tiles, send_list, clip_weight, kernel_dilated, kernel_mix, kernel_down, kernel_proj,
    kernel_teacher, alpha_one, alpha_two, alpha_three, alpha_teacher,
):
    routes = send_list.reshape(64, 2).T.reshape(128, 1)
    lat, total = whole(
        kernel_teacher, kernel_down, kernel_proj, kernel_dilated, kernel_mix, clip_weight,
        routes,
        student_tiles.reshape(2048, 256),
        teacher_tiles.reshape(2048, 512),
        [a.reshape(1, -1) for a in (alpha_one, alpha_two, alpha_three, alpha_teacher)],
    )
    total = total.reshape(96, 128)
    g_down = total[0:64].reshape(4, 16, 128).transpose(1, 0, 2).reshape(-1)
    return (
        lat.reshape(128, 2, 1024),
        total[64:78].reshape(-1),
        total[78:80].reshape(-1),
        g_down,
        total[80:96].reshape(-1),
    )


def solution(mesh):
    both = P(("dp", "fsdp"))
    return jax.shard_map(
        on_device,
        mesh=mesh,
        in_specs=(
            P(("dp", "fsdp"), None, None),
            P(("dp", "fsdp"), None, None),
            P("dp", "fsdp", None),
            both,
            P("fsdp", None),
            P("fsdp", None),
            P("fsdp", None),
            P("fsdp", None),
            P(None, "fsdp", None),
            P(),
            P(),
            P(),
            P(),
        ),
        out_specs=(P(("dp", "fsdp"), None, None), both, both, both, both),
        check_vma=False,
    )
```
